32 devices in a mesh: rep: 1, seq: 16 (over z, y, core), head: 2 (over x).
Axes of the slice: x: 2, y: 2, z: 4, core: 2. Of those that a mesh axis runs over, the one named last changes fastest.
Arguments:
- states: bfloat16 [256, 8192], P('rep', 'seq'), may hold values from -6 to 6
- w_query: bfloat16 [8192, 8192], P('seq', 'head'), may hold values from -0.0625 to 0.0625
- w_key: bfloat16 [8192, 1024], P('seq', 'head'), may hold values from -0.3125 to 0.3125
- w_value: bfloat16 [8192, 1024], P('seq', 'head'), may hold values from -0.25 to 0.25
- w_out: bfloat16 [8192, 8192], P('head', 'seq'), may hold values from -0.09375 to 0.09375
- key_cache: bfloat16 [2, 8192, 1024], P('rep', 'seq', 'head'), may hold values from -480 to 480
- value_cache: bfloat16 [2, 8192, 1024], P('rep', 'seq', 'head'), may hold values from -24 to 24
- parents: int32 [2, 128], P('rep'), may hold values from 0 to 126, as said below
- cache_lengths: int32 [2], P('rep'), may hold values from 2048 to 8192, as said below
Outputs:
- attended: bfloat16 [256, 8192], P('rep', ('seq', 'head'))
The draws below stay inside these ranges and needn't reach their ends.
Inputs may be any that keep to these rules, and one draw needn't show every extreme that they name: parents[t, 0] = 0, parents[t, i] < i for i >= 1, and the last node's parent is node 126. `cache_lengths`: at least one sequence fills all 8192 positions.
All inputs are finite; a program needn't handle non-finite values.
Results may differ from the reference program's by a relative error of at most 0.014.
The reference program's roundings to bfloat16 on the way (of `weights` and `attention`) count: a program that leaves them out, or rounds other values in their place, can miss the bound.
Values may be sent and summed in bfloat16 or wider, within the bound.
No kernel may reach another device: no remote copies, remote signals or barrier semaphores. Data moves between devices by JAX's collectives and lax.ppermute only.
A program may use at most 320 MiB of HBM per device.

```python
import jax
import jax.numpy as jnp
from jax import lax

D = 8192
HEADS = 64
KV_HEADS = 8
HEAD_DIM = 128
TREE = 128
TREES = 2
CACHE = 8192
ROWS = 256


def draw_key_cache(key, part):
    base = 2.0 * jax.random.normal(jax.random.fold_in(key, 11), (TREES, CACHE, KV_HEADS * HEAD_DIM), jnp.float32)
    base = jnp.clip(base, -12.0, 12.0)
    return base.astype(jnp.bfloat16)


def draw_parents(key, part):
    index = jnp.arange(TREE, dtype=jnp.int32)[None, :]
    raw = jax.random.randint(jax.random.fold_in(key, 21), (TREES, TREE), 0, 1 << 30)
    chain = jax.random.randint(jax.random.fold_in(key, 22), (TREES, TREE), 0, 2)
    earlier = raw % jnp.maximum(index, 1)
    pick = jnp.where(chain == 1, index - 1, earlier)
    pick = jnp.where(index == TREE - 1, index - 1, pick)
    return jnp.where(index == 0, 0, pick).astype(jnp.int32)


def draw_cache_lengths(key, part):
    other = jax.random.randint(jax.random.fold_in(key, 31), (TREES,), CACHE // 4, CACHE + 1)
    which = jax.random.randint(jax.random.fold_in(key, 32), (), 0, TREES)
    return jnp.where(jnp.arange(TREES, dtype=jnp.int32) == which, CACHE, other).astype(jnp.int32)


def shard_levels(own_key, shape, split, smallest, largest):
    def one(dim, blocks):
        draws = jax.random.uniform(jax.random.fold_in(jax.random.fold_in(own_key, 6), dim), (blocks,), jnp.float32, smallest / len(split), largest / len(split))
        return jnp.repeat(jnp.exp(draws), shape[dim] // blocks).reshape((-1,) + (1,) * (len(shape) - dim - 1))

    gain = one(*split[0])
    for cut in split[1:]:
        gain = gain * one(*cut)
    return gain


def normal_values(own_key, shape, spread, most, shards=(), kind=jnp.bfloat16):
    values = jax.random.normal(own_key, shape, jnp.float32) * spread
    if len(shards) > 0:
        values = shard_levels(own_key, shape, shards, -0.22, 0.18) * values
    return jnp.clip(values, min=-most, max=most).astype(kind)


def setup_inputs(seed: int = 0, part: int = 0) -> dict:
    key_list = jax.random.split(jax.random.key(seed), 10)
    own_keys = jax.random.split(jax.random.fold_in(key_list[9], part), 10)
    return {
        "states": normal_values(own_keys[0], (ROWS, D), 1.0, 6.0, ((1, 16),)),
        "w_query": normal_values(key_list[1], (D, HEADS * HEAD_DIM), D ** -0.5, 0.0625, ((0, 16), (1, 2))),
        "w_key": normal_values(key_list[2], (D, KV_HEADS * HEAD_DIM), (D // 25) ** -0.5, 0.3125, ((0, 16), (1, 2))),
        "w_value": normal_values(key_list[3], (D, KV_HEADS * HEAD_DIM), (D // 16) ** -0.5, 0.25, ((0, 16), (1, 2))),
        "w_out": normal_values(key_list[4], (HEADS * HEAD_DIM, D), (32 * HEAD_DIM) ** -0.5, 0.09375, ((0, 2), (1, 16))),
        "key_cache": draw_key_cache(jax.random.fold_in(jax.random.fold_in(key_list[9], part), 71), part),
        "value_cache": normal_values(own_keys[6], (TREES, CACHE, KV_HEADS * HEAD_DIM), 4.0, 24.0, ((1, 16), (2, 2))),
        "parents": draw_parents(jax.random.fold_in(jax.random.fold_in(key_list[9], part), 71), part),
        "cache_lengths": draw_cache_lengths(jax.random.fold_in(jax.random.fold_in(key_list[9], part), 71), part),
    }


rope_base = 500000.0
neg_big = -1.0e30


def ancestry(parents):
    count = parents.shape[1]
    ident = jnp.eye(count, dtype=jnp.float32)
    onehot = (parents[:, :, None] == jnp.arange(count, dtype=jnp.int32)[None, None, :]).astype(jnp.float32)
    reach = jnp.minimum(ident[None] + onehot, 1.0)
    for level in range(max(1, (count - 1).bit_length())):
        reach = jnp.minimum(jnp.einsum("tij,tjk->tik", reach, reach, precision=lax.Precision.HIGHEST), 1.0)
    return reach


def rotate(values, position):
    count = values.shape[0]
    half = HEAD_DIM // 2
    shaped = values.reshape(count, -1, HEAD_DIM)
    freq = rope_base ** (-(jnp.arange(half, dtype=jnp.float32) * 2.0 / HEAD_DIM))
    angle = position[:, None] * freq[None, :]
    cosine = jnp.cos(angle)[:, None, :]
    sine = jnp.sin(angle)[:, None, :]
    first = shaped[..., :half]
    second = shaped[..., half:]
    turned = jnp.concatenate([first * cosine - second * sine, second * cosine + first * sine], -1)
    return turned.reshape(count, -1)


def combine(left, right):
    top = jnp.maximum(left[0], right[0])
    scale_left = jnp.exp(left[0] - top)
    scale_right = jnp.exp(right[0] - top)
    return (top, left[1] * scale_left + right[1] * scale_right,
            left[2] * scale_left[..., None] + right[2] * scale_right[..., None])


def rounded(weights):
    return lax.optimization_barrier(weights.astype(jnp.bfloat16)).astype(jnp.float32)


def reference(states, w_query, w_key, w_value, w_out, key_cache, value_cache, parents, cache_lengths):
    q_raw = jnp.dot(states, w_query, preferred_element_type=jnp.float32)
    k_raw = jnp.dot(states, w_key, preferred_element_type=jnp.float32)
    v_raw = jnp.dot(states, w_value, preferred_element_type=jnp.float32)
    reach = ancestry(parents)
    position = (cache_lengths.astype(jnp.float32)[:, None] + jnp.sum(reach, -1) - 1.0).reshape(-1)
    queries = rotate(q_raw, position).astype(jnp.bfloat16)
    new_keys = rotate(k_raw, position).astype(jnp.bfloat16)
    new_values = v_raw.astype(jnp.bfloat16)
    group = HEADS // KV_HEADS
    scale = HEAD_DIM ** -0.5
    allowed = (jnp.eye(TREES, dtype=jnp.float32)[:, None, :, None] * reach[:, :, None, :]).reshape(ROWS, ROWS) > 0.5
    keys_new = new_keys.astype(jnp.float32).reshape(ROWS, KV_HEADS, HEAD_DIM)
    values_new = new_values.astype(jnp.float32).reshape(ROWS, KV_HEADS, HEAD_DIM)
    block = min(CACHE, 8192)
    count = CACHE // block
    results = []
    for tree in range(TREES):
        query = queries[tree * TREE:(tree + 1) * TREE].astype(jnp.float32).reshape(TREE, KV_HEADS, group, HEAD_DIM)
        keys = key_cache[tree].reshape(count, block, KV_HEADS, HEAD_DIM)
        values = value_cache[tree].reshape(count, block, KV_HEADS, HEAD_DIM)
        length = cache_lengths[tree]

        def step(carry, inputs):
            key_block, value_block, first = inputs
            valid = (first + jnp.arange(block, dtype=jnp.int32)) < length
            scores = jnp.einsum("rkgd,nkd->rkgn", query, key_block.astype(jnp.float32),
                                precision=lax.Precision.HIGHEST) * scale
            scores = jnp.where(valid, scores, neg_big)
            top = jnp.maximum(carry[0], jnp.max(scores, -1))
            weights = jnp.where(valid, jnp.exp(scores - top[..., None]), 0.0)
            shrink = jnp.exp(carry[0] - top)
            mass = carry[1] * shrink + jnp.sum(weights, -1)
            acc = carry[2] * shrink[..., None] + jnp.einsum(
                "rkgn,nkd->rkgd", rounded(weights), value_block.astype(jnp.float32), precision=lax.Precision.HIGHEST)
            return (top, mass, acc), None

        init = (jnp.full((TREE, KV_HEADS, group), neg_big, jnp.float32),
                jnp.zeros((TREE, KV_HEADS, group), jnp.float32),
                jnp.zeros((TREE, KV_HEADS, group, HEAD_DIM), jnp.float32))
        firsts = jnp.arange(count, dtype=jnp.int32) * block
        state, _ = lax.scan(step, init, (keys, values, firsts))
        mask = allowed[tree * TREE:(tree + 1) * TREE][:, None, None, :]
        scores = jnp.einsum("rkgd,nkd->rkgn", query, keys_new, precision=lax.Precision.HIGHEST) * scale
        scores = jnp.where(mask, scores, neg_big)
        top = jnp.max(scores, -1)
        weights = jnp.where(mask, jnp.exp(scores - top[..., None]), 0.0)
        tree_part = (top, jnp.sum(weights, -1),
                     jnp.einsum("rkgn,nkd->rkgd", rounded(weights), values_new, precision=lax.Precision.HIGHEST))
        total = combine(state, tree_part)
        results.append((total[2] / total[1][..., None]).reshape(TREE, HEADS * HEAD_DIM))
    attention = jnp.concatenate(results, 0).astype(jnp.bfloat16)
    return jnp.dot(attention, w_out, preferred_element_type=jnp.float32).astype(jnp.bfloat16)
```

```python
import functools

import jax
import jax.numpy as jnp
from jax import lax
from jax.experimental import pallas as pl
from jax.experimental.pallas import tpu as pltpu
from jax.sharding import PartitionSpec as P


HEAD_DIM = 128
rope_base = 500000.0
neg_big = -1e30
log2_e = 1.4426950408889634

VMEM = pl.BlockSpec(memory_space=pltpu.VMEM)
SMEM = pl.BlockSpec(memory_space=pltpu.SMEM)


def room(mib):
    return pltpu.CompilerParams(vmem_limit_bytes=mib * 1024 * 1024)


def bits_of(count):
    return max(0, (count - 1).bit_length())


def reverse_bits(value, width):
    out = 0
    for bit in range(width):
        out = out | (((value >> bit) & 1) << (width - 1 - bit))
    return out


def swap(value, mask, size):
    return lax.ppermute(value, "seq", [(i, i ^ mask) for i in range(size)])


def dot_t(left, right):
    return lax.dot_general(left, right, (((1,), (1,)), ((), ())), preferred_element_type=jnp.float32)


def place_of(splits, trees):
    me = lax.axis_index("seq").astype(jnp.int32)
    split_bits = bits_of(splits)
    return me & (splits - 1), (me >> split_bits) & (trees - 1), me >> (split_bits + bits_of(trees))


def pack_kernel(splits, trees, key_ref, value_ref, *outs):
    _, tree, head = place_of(splits, trees)
    for unit, out in enumerate(outs):
        source = (unit & (trees - 1)) ^ tree
        lanes = pl.ds(pl.multiple_of(((unit >> bits_of(trees)) ^ head) * HEAD_DIM, HEAD_DIM), HEAD_DIM)
        out[0] = key_ref[source, :, lanes]
        out[1] = value_ref[source, :, lanes]


def project_kernel(splits, trees, states, wq, wk, wv, keep, low_send, high_send):
    my_part, my_tree, my_head = place_of(splits, trees)
    heads, share = keep.shape[1:3]
    width = bits_of(splits)
    rows = []
    for part in range(splits):
        for tree in range(trees):
            row = ((tree ^ my_tree) * splits + (reverse_bits(part, width) ^ my_part)) * share
            rows.append(states[pl.ds(pl.multiple_of(row, share), share), :])
    left = jnp.concatenate(rows, 0)
    for head in range(heads):
        source = reverse_bits(head, bits_of(heads)) ^ my_head
        low = 0
        for weight in (wq, wk, wv):
            size = weight.shape[1] // heads
            lanes = pl.ds(pl.multiple_of(source * size, size), size)
            out = jnp.dot(left, weight[:, lanes], preferred_element_type=jnp.float32)
            row = 0
            for target in (keep, low_send, high_send):
                count = target.shape[0]
                piece = out[row : row + count * share].reshape(count, share, size)
                target[:, head, :, low : low + size] = piece
                row += count * share
            low += size


def lane_blocks(value):
    return [value[:, low : low + HEAD_DIM] for low in range(0, value.shape[1], HEAD_DIM)]


def scores_of(query, keys, scores, meta, offset, top):
    span = keys.shape[1]
    length = meta[4]

    def body(i, top):
        piece = dot_t(query[...], keys[i])
        place = meta[offset + i] + lax.broadcasted_iota(jnp.int32, (1, span), 1)
        piece = piece + jnp.where(place < length, 0.0, neg_big)
        scores[i] = piece
        return functools.reduce(jnp.maximum, lane_blocks(piece), top)

    return lax.fori_loop(0, keys.shape[0], body, top)


def weigh(scores, values, top, mass, acc):
    rate = HEAD_DIM**-0.5 * log2_e

    def body(i, _):
        weight = jnp.exp2((scores[i] - top) * rate)
        mass[...] += functools.reduce(jnp.add, lane_blocks(weight))
        acc[...] += jnp.dot(weight.astype(jnp.bfloat16), values[i], preferred_element_type=jnp.float32)
        return 0

    lax.fori_loop(0, values.shape[0], body, 0)


def cache_kernel(count, group, offset, meta, raw, cosine, sine, *refs):
    chunks = refs[:count]
    query, top_out, mass, acc, keys, values, scores = refs[count:]
    share = raw.shape[0]
    for head in range(group):
        value = raw[:, head * HEAD_DIM : (head + 1) * HEAD_DIM]
        value = value * cosine[...] + pltpu.roll(value, HEAD_DIM // 2, 1) * sine[...]
        query[head * share : (head + 1) * share, :] = value.astype(query.dtype)
    for i, chunk in enumerate(chunks):
        keys[i] = chunk[0]
        values[i] = chunk[1]
    top = jnp.full(top_out.shape, neg_big, jnp.float32)
    top = scores_of(query, keys, scores, meta, offset, top)
    top = jnp.max(top, 1, keepdims=True)
    mass[...] = jnp.zeros(mass.shape, jnp.float32)
    acc[...] = jnp.zeros(acc.shape, jnp.float32)
    weigh(scores, values, top, mass, acc)
    top_out[...] = jnp.broadcast_to(top, top_out.shape)


def last_kernel(count, pieces, group, offset, meta, query, *refs):
    chunks = refs[:count]
    fresh = refs[count : count + pieces]
    bias, top_in, mass_in, acc_in, out, keys, values, scores, nodes, mass, acc = refs[count + pieces :]
    rate = HEAD_DIM**-0.5 * log2_e
    rows = query.shape[0]
    share = rows // group
    for i, chunk in enumerate(chunks):
        keys[i] = chunk[0]
        values[i] = chunk[1]
    for i, piece in enumerate(fresh):
        place = pl.ds(pl.multiple_of((meta[0] ^ i) * share, share), share)
        nodes[0, place, :] = piece[0]
        nodes[1, place, :] = piece[1]
    tree = dot_t(query[...], nodes[0])
    tree = (tree.reshape(group, share, -1) + bias[...][None]).reshape(rows, -1)
    top = functools.reduce(jnp.maximum, lane_blocks(tree), top_in[...])
    top = scores_of(query, keys, scores, meta, offset, top)
    top = jnp.max(top, 1, keepdims=True)
    shrink = jnp.exp2((top_in[...] - top) * rate)
    weight = jnp.exp2((tree - top) * rate)
    mass[...] = mass_in[...] * shrink + functools.reduce(jnp.add, lane_blocks(weight))
    acc[...] = acc_in[...] * shrink + jnp.dot(
        weight.astype(jnp.bfloat16), nodes[1], preferred_element_type=jnp.float32
    )
    weigh(scores, values, top, mass, acc)
    total = jnp.sum(mass[...], 1, keepdims=True)
    result = (acc[...] / total).astype(out.dtype)
    for head in range(group):
        out[:, head * HEAD_DIM : (head + 1) * HEAD_DIM] = result[head * share : (head + 1) * share]


def out_kernel(splits, trees, heads, step, meta, *refs):
    blocks = refs[: splits * trees * heads]
    weight, out = refs[splits * trees * heads :]
    share, depth = blocks[0].shape
    width = out.shape[1]
    if weight.shape[1] == width:
        column = slice(None)
    else:
        column = pl.ds(pl.multiple_of((meta[3] ^ step) * width, width), width)
    total = None
    for head in range(heads):
        left = jnp.concatenate(
            [blocks[(head * trees + tree) * splits + part][...] for tree in range(trees) for part in range(splits)], 0
        )
        deep = pl.ds(pl.multiple_of((head ^ meta[2]) * depth, depth), depth)
        term = jnp.dot(left, weight[deep, column], preferred_element_type=jnp.float32)
        total = term if total is None else total + term
    for tree in range(trees):
        for part in range(splits):
            row = ((tree ^ meta[1]) * splits + (part ^ meta[0])) * share
            low = (tree * splits + part) * share
            out[pl.ds(pl.multiple_of(row, share), share), :] = total[low : low + share].astype(out.dtype)


def reach_of(parent):
    count = parent.shape[0]
    spots = jnp.arange(count, dtype=jnp.int32)
    reach = ((parent[:, None] == spots[None, :]) | (spots[:, None] == spots[None, :])).astype(jnp.bfloat16)
    for _ in range(max(1, (count - 1).bit_length())):
        reach = jnp.minimum(jnp.dot(reach, reach, preferred_element_type=jnp.float32), 1.0).astype(jnp.bfloat16)
    return reach.astype(jnp.float32)


def local(size, sides, states, w_query, w_key, w_value, w_out, key_cache, value_cache, parents, cache_lengths):
    trees, tree_rows = parents.shape
    rows = trees * tree_rows
    span = key_cache.shape[1]
    heads = key_cache.shape[2] // HEAD_DIM
    group = w_query.shape[1] // HEAD_DIM // heads
    units = trees * heads
    splits = size // units
    share = tree_rows // splits
    split_bits, tree_bits = bits_of(splits), bits_of(trees)
    width = (group + 2) * HEAD_DIM
    f32, bf16 = jnp.float32, jnp.bfloat16
    shape = jax.ShapeDtypeStruct

    me = lax.axis_index("seq").astype(jnp.int32)
    side = lax.axis_index("head").astype(jnp.int32)
    my_part = me & (splits - 1)
    my_tree = (me >> split_bits) & (trees - 1)
    my_head = me >> (split_bits + tree_bits)

    order = sorted(
        range(1, units), key=lambda u: (-(u & (trees - 1)), -bits_of((u >> tree_bits) + 1), u)
    )
    masks = [unit * splits + part for unit in [0] + order for part in range(splits)]
    length = lax.dynamic_index_in_dim(cache_lengths, my_tree, 0, False)
    meta = jnp.stack(
        [my_part, my_tree, my_head, side, length, me] + [(me ^ mask) * span for mask in masks]
    )
    near = len(masks) // 2

    packed = pl.pallas_call(
        functools.partial(pack_kernel, splits, trees),
        out_shape=[shape((2, span, HEAD_DIM), bf16)] * units,
        in_specs=[VMEM, VMEM],
        out_specs=[VMEM] * units,
        name="pack",
    )(key_cache, value_cache)
    held = {0: packed[0]}
    for unit in order:
        held[unit] = swap(packed[unit], unit * splits, size)

    groups = splits * trees
    project = pl.pallas_call(
        functools.partial(project_kernel, splits, trees),
        out_shape=[shape((part, heads, share, width), f32) for part in (groups // 2, groups // 4, groups // 4)],
        in_specs=[VMEM] * 4,
        out_specs=[VMEM] * 3,
        name="project",
        compiler_params=room(12),
    )
    keep, low_send, high_send = project(states, w_query, w_key, w_value)
    keep, low_send, high_send = [item.reshape(-1, share, width) for item in (keep, low_send, high_send)]
    steps = bits_of(size)
    rest = jnp.zeros((), f32)
    for bit in range(steps - 1):
        high = swap(high_send, 1 << bit, size)
        low = swap(low_send, 1 << bit, size)
        half = keep.shape[0] // 2
        if bit:
            high, rest = lax.optimization_barrier((high, rest))
            keep = keep + rest.astype(f32)
        send = (keep[half:] + high.astype(f32)).astype(jnp.float16)
        keep, rest = keep[:half], low
        low_send, high_send = send[: half // 2], send[half // 2 :]
    high = swap(send, 1 << (steps - 1), size)
    high, rest = lax.optimization_barrier((high, rest))
    raw = (keep + rest.astype(f32) + high.astype(f32))[0]
    w_out, raw = lax.optimization_barrier((w_out, raw))

    reach = reach_of(lax.dynamic_index_in_dim(parents, my_tree, 0, False))
    reach_rows = lax.dynamic_slice_in_dim(reach, my_part * share, share, 0)
    position = length.astype(f32) + jnp.sum(reach_rows, -1) - 1.0
    half_dim = HEAD_DIM // 2
    freq = rope_base ** (-(jnp.arange(half_dim, dtype=f32) * 2.0 / HEAD_DIM))
    angle = position[:, None] * freq[None, :]
    cosine = jnp.cos(angle)
    sine = jnp.sin(angle)
    cosine = jnp.concatenate([cosine, cosine], -1)
    sine = jnp.concatenate([-sine, sine], -1)
    bias = jnp.where(reach_rows > 0.5, 0.0, neg_big)

    raw_key = raw[:, group * HEAD_DIM : (group + 1) * HEAD_DIM]
    new_key = raw_key * cosine + jnp.roll(raw_key, half_dim, 1) * sine
    fresh = [jnp.stack([new_key.astype(bf16), raw[:, (group + 1) * HEAD_DIM :].astype(bf16)])]
    chunks = {unit: [held[unit]] for unit in held}
    for bit in range(split_bits):
        fresh = fresh + [swap(item, 1 << bit, size) for item in fresh]
        for unit in chunks:
            chunks[unit] = chunks[unit] + [swap(item, 1 << bit, size) for item in chunks[unit]]
    chunks = [item for unit in [0] + order for item in chunks[unit]]

    count = group * share
    query, top, mass, acc = pl.pallas_call(
        functools.partial(cache_kernel, near, group, 6),
        out_shape=[shape((count, HEAD_DIM), bf16)] + [shape((count, HEAD_DIM), f32)] * 3,
        in_specs=[SMEM] + [VMEM] * (3 + near),
        out_specs=[VMEM] * 4,
        scratch_shapes=[
            pltpu.VMEM((near, span, HEAD_DIM), bf16),
            pltpu.VMEM((near, span, HEAD_DIM), bf16),
            pltpu.VMEM((near, count, span), f32),
        ],
        name="cache",
        compiler_params=room(20),
    )(meta, raw, cosine, sine, *chunks[:near])

    far = len(masks) - near
    block = pl.pallas_call(
        functools.partial(last_kernel, far, splits, group, 6 + near),
        out_shape=shape((share, group * HEAD_DIM), bf16),
        in_specs=[SMEM] + [VMEM] * (1 + far + splits + 4),
        out_specs=VMEM,
        scratch_shapes=[
            pltpu.VMEM((far, span, HEAD_DIM), bf16),
            pltpu.VMEM((far, span, HEAD_DIM), bf16),
            pltpu.VMEM((far, count, span), f32),
            pltpu.VMEM((2, tree_rows, HEAD_DIM), bf16),
            pltpu.VMEM((count, HEAD_DIM), f32),
            pltpu.VMEM((count, HEAD_DIM), f32),
        ],
        name="last",
        compiler_params=room(20),
    )(meta, query, *chunks[near:], *fresh, bias, top, mass, acc)

    blocks = [block] + [swap(block, i * splits * trees, size) for i in range(1, heads)]
    blocks = [
        item if i == 0 else swap(item, i * splits, size) for item in blocks for i in range(trees)
    ]
    blocks = [[item] for item in blocks]
    for bit in range(split_bits):
        blocks = [item + [swap(piece, 1 << bit, size) for piece in item] for item in blocks]
    blocks = [piece for item in blocks for piece in item]

    out_width = w_out.shape[1] // sides
    if sides == 2:
        order = [1, 0]
    else:
        order = list(range(1, sides)) + [0]

    def product(step, dtype):
        weight = w_out
        if out_width % HEAD_DIM:
            weight = lax.dynamic_slice_in_dim(w_out, (side ^ step) * out_width, out_width, 1)
        return pl.pallas_call(
            functools.partial(out_kernel, splits, trees, heads, step),
            out_shape=shape((rows, out_width), dtype),
            in_specs=[SMEM] + [VMEM] * (len(blocks) + 1),
            out_specs=VMEM,
            name="output",
            compiler_params=room(12),
        )(meta, *blocks, weight)

    total = None
    arrived = []
    for step in order:
        if step:
            arrived.append(
                lax.ppermute(product(step, bf16), "head", [(i, i ^ step) for i in range(sides)])
            )
        else:
            total = product(step, f32)
    for item in arrived:
        total = total + item.astype(f32)
    return total.astype(bf16)


def solution(mesh):
    placed = (
        P("rep", "seq"),
        P("seq", "head"),
        P("seq", "head"),
        P("seq", "head"),
        P("head", "seq"),
        P("rep", "seq", "head"),
        P("rep", "seq", "head"),
        P("rep", None),
        P("rep"),
    )
    return jax.shard_map(
        functools.partial(local, mesh.shape["seq"], mesh.shape["head"]),
        mesh=mesh,
        in_specs=placed,
        out_specs=P("rep", ("seq", "head")),
        check_vma=False,
    )
```

```python
import functools

import jax
import jax.numpy as jnp
from jax import lax
from jax.experimental import pallas as pl
from jax.experimental.pallas import tpu as pltpu
from jax.sharding import PartitionSpec as P


HEAD_DIM = 128
rope_base = 500000.0
neg_big = -1e30
log2_e = 1.4426950408889634

HBM = pl.BlockSpec(memory_space=pltpu.HBM)
VMEM = pl.BlockSpec(memory_space=pltpu.VMEM)


def room(mib):
    return pltpu.CompilerParams(vmem_limit_bytes=mib * 1024 * 1024)


def bits_of(count):
    return max(0, (count - 1).bit_length())


def reverse_bits(value, width):
    out = 0
    for bit in range(width):
        out = out | (((value >> bit) & 1) << (width - 1 - bit))
    return out


def swap(value, mask, size):
    return lax.ppermute(value, "seq", [(i, i ^ mask) for i in range(size)])


def dot_t(left, right):
    return lax.dot_general(left, right, (((1,), (1,)), ((), ())), preferred_element_type=jnp.float32)


def place_of(splits, trees):
    me = lax.axis_index("seq").astype(jnp.int32)
    split_bits = bits_of(splits)
    return me & (splits - 1), (me >> split_bits) & (trees - 1), me >> (split_bits + bits_of(trees))


def pack_kernel(splits, trees, units, key_ref, value_ref, *refs):
    outs, sems = refs[:-1], refs[-1]
    _, tree, head = place_of(splits, trees)
    copies = []
    for unit, out in zip(units, outs):
        source = (unit & (trees - 1)) ^ tree
        lanes = pl.ds(pl.multiple_of(((unit >> bits_of(trees)) ^ head) * HEAD_DIM, HEAD_DIM), HEAD_DIM)
        for i, ref in enumerate((key_ref, value_ref)):
            copies.append(pltpu.make_async_copy(ref.at[source, :, lanes], out.at[i], sems.at[len(copies)]))
    for copy in copies:
        copy.start()
    for copy in copies:
        copy.wait()


def project_kernel(splits, trees, heads, states, wq, wk, wv, *targets):
    my_part, my_tree, my_head = place_of(splits, trees)
    share = targets[0].shape[1]
    width = bits_of(splits)
    rows = []
    for part in range(splits):
        for tree in range(trees):
            row = ((tree ^ my_tree) * splits + (reverse_bits(part, width) ^ my_part)) * share
            rows.append(states[pl.ds(pl.multiple_of(row, share), share), :])
    left = jnp.concatenate(rows, 0)
    for head in range(heads):
        source = reverse_bits(head, bits_of(heads)) ^ my_head
        low = 0
        for weight in (wq, wk, wv):
            size = weight.shape[1] // heads
            lanes = pl.ds(pl.multiple_of(source * size, size), size)
            out = jnp.dot(left, weight[:, lanes], preferred_element_type=jnp.float32)
            for group in range(splits * trees):
                spot = group * heads + head
                for target in targets:
                    if spot < target.shape[0]:
                        target[spot, :, low : low + size] = out[group * share : (group + 1) * share]
                        break
                    spot -= target.shape[0]
            low += size


def lane_blocks(value):
    return [value[:, low : low + HEAD_DIM] for low in range(0, value.shape[1], HEAD_DIM)]


def scores_of(query, keys, scores, filled, top):
    def body(i, top):
        piece = dot_t(query[...], keys[i])
        piece = piece + filled[pl.ds(i, 1), :]
        scores[i] = piece
        return functools.reduce(jnp.maximum, lane_blocks(piece), top)

    return lax.fori_loop(0, keys.shape[0], body, top)


def weigh(scores, values, top, mass, acc):
    rate = HEAD_DIM**-0.5 * log2_e

    def body(i, _):
        weight = jnp.exp2((scores[i] - top) * rate)
        mass[...] += functools.reduce(jnp.add, lane_blocks(weight))
        acc[...] += jnp.dot(weight.astype(jnp.bfloat16), values[i], preferred_element_type=jnp.float32)
        return 0

    lax.fori_loop(0, values.shape[0], body, 0)


def cache_kernel(count, group, filled, raw, cosine, sine, *refs):
    chunks = refs[:count]
    query, top_out, mass, acc, keys, values, scores = refs[count:]
    share = raw.shape[0]
    for head in range(group):
        value = raw[:, head * HEAD_DIM : (head + 1) * HEAD_DIM]
        value = value * cosine[...] + pltpu.roll(value, HEAD_DIM // 2, 1) * sine[...]
        query[head * share : (head + 1) * share, :] = value.astype(query.dtype)
    for i, chunk in enumerate(chunks):
        keys[i] = chunk[0]
        values[i] = chunk[1]
    top = jnp.full(top_out.shape, neg_big, jnp.float32)
    top = scores_of(query, keys, scores, filled, top)
    top = jnp.max(top, 1, keepdims=True)
    mass[...] = jnp.zeros(mass.shape, jnp.float32)
    acc[...] = jnp.zeros(acc.shape, jnp.float32)
    weigh(scores, values, top, mass, acc)
    top_out[...] = jnp.broadcast_to(top, top_out.shape)


def last_kernel(count, pieces, group, filled, query, *refs):
    chunks = refs[:count]
    fresh = refs[count : count + pieces]
    bias, top_in, mass_in, acc_in, out, keys, values, scores, nodes, mass, acc = refs[count + pieces :]
    rate = HEAD_DIM**-0.5 * log2_e
    rows = query.shape[0]
    share = rows // group
    for i, chunk in enumerate(chunks):
        keys[i] = chunk[0]
        values[i] = chunk[1]
    mine = lax.axis_index("seq").astype(jnp.int32) & (pieces - 1)
    for i, piece in enumerate(fresh):
        place = pl.ds(pl.multiple_of((mine ^ i) * share, share), share)
        nodes[0, place, :] = piece[0]
        nodes[1, place, :] = piece[1]
    tree = dot_t(query[...], nodes[0])
    tree = (tree.reshape(group, share, -1) + bias[...][None]).reshape(rows, -1)
    top = functools.reduce(jnp.maximum, lane_blocks(tree), top_in[...])
    top = scores_of(query, keys, scores, filled, top)
    top = jnp.max(top, 1, keepdims=True)
    shrink = jnp.exp2((top_in[...] - top) * rate)
    weight = jnp.exp2((tree - top) * rate)
    mass[...] = mass_in[...] * shrink + functools.reduce(jnp.add, lane_blocks(weight))
    acc[...] = acc_in[...] * shrink + jnp.dot(
        weight.astype(jnp.bfloat16), nodes[1], preferred_element_type=jnp.float32
    )
    weigh(scores, values, top, mass, acc)
    total = jnp.sum(mass[...], 1, keepdims=True)
    result = (acc[...] / total).astype(out.dtype)
    for head in range(group):
        out[:, head * HEAD_DIM : (head + 1) * HEAD_DIM] = result[head * share : (head + 1) * share]


def out_kernel(splits, trees, heads, step, *refs):
    my_part, my_tree, my_head = place_of(splits, trees)
    blocks = refs[: splits * trees * heads]
    weight, out = refs[splits * trees * heads :]
    share, depth = blocks[0].shape
    width = out.shape[1]
    if weight.shape[1] == width:
        column = slice(None)
    else:
        column = pl.ds(pl.multiple_of((lax.axis_index("head").astype(jnp.int32) ^ step) * width, width), width)
    total = None
    for head in range(heads):
        left = jnp.concatenate(
            [blocks[(head * trees + tree) * splits + part][...] for tree in range(trees) for part in range(splits)], 0
        )
        deep = pl.ds(pl.multiple_of((head ^ my_head) * depth, depth), depth)
        term = jnp.dot(left, weight[deep, column], preferred_element_type=jnp.float32)
        total = term if total is None else total + term
    for tree in range(trees):
        for part in range(splits):
            row = ((tree ^ my_tree) * splits + (part ^ my_part)) * share
            low = (tree * splits + part) * share
            out[pl.ds(pl.multiple_of(row, share), share), :] = total[low : low + share].astype(out.dtype)


def reach_of(parent):
    count = parent.shape[0]
    spots = jnp.arange(count, dtype=jnp.int32)
    reach = ((parent[:, None] == spots[None, :]) | (spots[:, None] == spots[None, :])).astype(jnp.bfloat16)
    for _ in range(max(1, (count - 1).bit_length())):
        reach = jnp.minimum(jnp.dot(reach, reach, preferred_element_type=jnp.float32), 1.0).astype(jnp.bfloat16)
    return reach.astype(jnp.float32)


def local(size, sides, states, w_query, w_key, w_value, w_out, key_cache, value_cache, parents, cache_lengths):
    trees, tree_rows = parents.shape
    rows = trees * tree_rows
    span = key_cache.shape[1]
    heads = key_cache.shape[2] // HEAD_DIM
    group = w_query.shape[1] // HEAD_DIM // heads
    units = trees * heads
    splits = size // units
    share = tree_rows // splits
    split_bits = bits_of(splits)
    width = (group + 2) * HEAD_DIM
    f32, bf16 = jnp.float32, jnp.bfloat16
    shape = jax.ShapeDtypeStruct

    me = lax.axis_index("seq").astype(jnp.int32)
    side = lax.axis_index("head").astype(jnp.int32)
    my_part = me & (splits - 1)
    my_tree = (me >> split_bits) & (trees - 1)

    steps = bits_of(size)
    pieces = [size // 2, size // 4, size // 4]
    project = pl.pallas_call(
        functools.partial(project_kernel, splits, trees, heads),
        out_shape=[shape((piece, share, width), f32) for piece in pieces],
        in_specs=[VMEM] * 4,
        out_specs=[VMEM] * len(pieces),
        name="project",
        compiler_params=room(12),
    )
    keep, low_send, high_send = project(states, w_query, w_key, w_value)
    rest = None
    for bit in range(steps - 1):
        high = swap(high_send, 1 << bit, size)
        low = swap(low_send, 1 << bit, size)
        if rest is not None:
            high, rest = lax.optimization_barrier((high, rest))
            keep = keep + rest.astype(f32)
        half = keep.shape[0] // 2
        send = (keep[half:] + high.astype(f32)).astype(jnp.float16)
        keep, rest = keep[:half], low
        if bit == 0:
            keep, rest = keep + low, None
        low_send, high_send = send[: half // 2], send[half // 2 :]
    high = swap(send, 1 << (steps - 1), size)
    high, rest = lax.optimization_barrier((high, rest))
    raw = (keep + rest.astype(f32) + high.astype(f32))[0]
    away = sorted(range(1, heads), key=lambda h: (h.bit_count() > 1, -h))
    order = [h * trees + t for h in away for t in range(1, trees)]
    order += [h * trees for h in away[:-1]]
    order += list(range(1, trees))
    order += [h * trees for h in away[-1:]]
    packed = pl.pallas_call(
        functools.partial(pack_kernel, splits, trees, [0] + order),
        out_shape=[shape((2, span, HEAD_DIM), bf16)] * units,
        in_specs=[HBM, HBM],
        out_specs=[VMEM] * units,
        scratch_shapes=[pltpu.SemaphoreType.DMA((2 * units,))],
        name="pack",
        compiler_params=room(60),
    )(key_cache, value_cache)
    held = {0: packed[0]}
    for spot, unit in enumerate(order):
        held[unit] = swap(packed[1 + spot], unit * splits, size)

    w_out, raw = lax.optimization_barrier((w_out, raw))

    length = lax.dynamic_index_in_dim(cache_lengths, my_tree, 0, False)
    masks = [unit * splits + part for unit in [0] + order for part in range(splits)]
    sources = jnp.stack([me ^ mask for mask in masks])
    places = sources[:, None] * span + jnp.arange(span, dtype=jnp.int32)[None, :]
    filled = jnp.where(places < length, 0.0, neg_big)
    near = len(masks) - splits
    reach = reach_of(lax.dynamic_index_in_dim(parents, my_tree, 0, False))
    reach_rows = lax.dynamic_slice_in_dim(reach, my_part * share, share, 0)
    position = length.astype(f32) + jnp.sum(reach_rows, -1) - 1.0
    half_dim = HEAD_DIM // 2
    freq = rope_base ** (-(jnp.arange(half_dim, dtype=f32) * 2.0 / HEAD_DIM))
    angle = position[:, None] * freq[None, :]
    cosine = jnp.cos(angle)
    sine = jnp.sin(angle)
    cosine = jnp.concatenate([cosine, cosine], -1)
    sine = jnp.concatenate([-sine, sine], -1)
    bias = jnp.where(reach_rows > 0.5, 0.0, neg_big)

    raw_key = raw[:, group * HEAD_DIM : (group + 1) * HEAD_DIM]
    new_key = raw_key * cosine + jnp.roll(raw_key, half_dim, 1) * sine
    fresh = [jnp.stack([new_key.astype(bf16), raw[:, (group + 1) * HEAD_DIM :].astype(bf16)])]
    for bit in range(split_bits):
        fresh = fresh + [swap(item, 1 << bit, size) for item in fresh]
    chunks = []
    for unit in [0] + order:
        pieces = [held[unit]]
        for bit in range(split_bits):
            pieces = pieces + [swap(item, 1 << bit, size) for item in pieces]
        chunks += pieces

    count = group * share
    attend = pl.pallas_call(
        functools.partial(cache_kernel, near, group),
        out_shape=[shape((count, HEAD_DIM), bf16)] + [shape((count, HEAD_DIM), f32)] * 3,
        in_specs=[VMEM] * (4 + near),
        out_specs=[VMEM] * 4,
        scratch_shapes=[
            pltpu.VMEM((near, span, HEAD_DIM), bf16),
            pltpu.VMEM((near, span, HEAD_DIM), bf16),
            pltpu.VMEM((near, count, span), f32),
        ],
        name="cache",
        compiler_params=room(30),
    )
    query, top, mass, acc = attend(filled[:near], raw, cosine, sine, *chunks[:near])

    far = len(masks) - near
    block = pl.pallas_call(
        functools.partial(last_kernel, far, splits, group),
        out_shape=shape((share, group * HEAD_DIM), bf16),
        in_specs=[VMEM] * (2 + far + splits + 4),
        out_specs=VMEM,
        scratch_shapes=[
            pltpu.VMEM((far, span, HEAD_DIM), bf16),
            pltpu.VMEM((far, span, HEAD_DIM), bf16),
            pltpu.VMEM((far, count, span), f32),
            pltpu.VMEM((2, tree_rows, HEAD_DIM), bf16),
            pltpu.VMEM((count, HEAD_DIM), f32),
            pltpu.VMEM((count, HEAD_DIM), f32),
        ],
        name="last",
        compiler_params=room(14),
    )(filled[near:], query, *chunks[near:], *fresh, bias, top, mass, acc)

    blocks = [block] + [swap(block, i * splits * trees, size) for i in range(1, heads)]
    blocks = [
        item if i == 0 else swap(item, i * splits, size) for item in blocks for i in range(trees)
    ]
    blocks = [[item] for item in blocks]
    for bit in range(split_bits):
        blocks = [item + [swap(piece, 1 << bit, size) for piece in item] for item in blocks]
    blocks = [piece for item in blocks for piece in item]

    out_width = w_out.shape[1] // sides
    if sides == 2:
        order = [1, 0]
    else:
        order = list(range(1, sides)) + [0]

    def product(step, dtype):
        weight = w_out
        if out_width % HEAD_DIM:
            weight = lax.dynamic_slice_in_dim(w_out, (side ^ step) * out_width, out_width, 1)
        return pl.pallas_call(
            functools.partial(out_kernel, splits, trees, heads, step),
            out_shape=shape((rows, out_width), dtype),
            in_specs=[VMEM] * (len(blocks) + 1),
            out_specs=VMEM,
            name="output",
            compiler_params=room(12),
        )(*blocks, weight)

    total = None
    arrived = []
    for step in order:
        if step:
            arrived.append(
                lax.ppermute(product(step, bf16), "head", [(i, i ^ step) for i in range(sides)])
            )
        else:
            total = product(step, f32)
    for item in arrived:
        total = total + item.astype(f32)
    return total.astype(bf16)


def solution(mesh):
    placed = (
        P("rep", "seq"),
        P("seq", "head"),
        P("seq", "head"),
        P("seq", "head"),
        P("head", "seq"),
        P("rep", "seq", "head"),
        P("rep", "seq", "head"),
        P("rep", None),
        P("rep"),
    )
    return jax.shard_map(
        functools.partial(local, mesh.shape["seq"], mesh.shape["head"]),
        mesh=mesh,
        in_specs=placed,
        out_specs=P("rep", ("seq", "head")),
        check_vma=False,
    )
```

```python
import functools

import jax
import jax.numpy as jnp
from jax import lax
from jax.experimental import pallas as pl
from jax.experimental.pallas import tpu as pltpu
from jax.sharding import PartitionSpec as P


HEAD_DIM = 128
rope_base = 500000.0
neg_big = -1e30
log2_e = 1.4426950408889634

HBM = pl.BlockSpec(memory_space=pltpu.HBM)
VMEM = pl.BlockSpec(memory_space=pltpu.VMEM)


def room(mib):
    return pltpu.CompilerParams(vmem_limit_bytes=mib * 1024 * 1024)


def bits_of(count):
    return max(0, (count - 1).bit_length())


def reverse_bits(value, width):
    out = 0
    for bit in range(width):
        out = out | (((value >> bit) & 1) << (width - 1 - bit))
    return out


def swap(value, mask, size):
    return lax.ppermute(value, "seq", [(i, i ^ mask) for i in range(size)])


def dot_t(left, right):
    return lax.dot_general(left, right, (((1,), (1,)), ((), ())), preferred_element_type=jnp.float32)


def place_of(splits, trees):
    me = lax.axis_index("seq").astype(jnp.int32)
    split_bits = bits_of(splits)
    return me & (splits - 1), (me >> split_bits) & (trees - 1), me >> (split_bits + bits_of(trees))


def pack_kernel(splits, trees, units, key_ref, value_ref, *refs):
    outs, sems = refs[:-1], refs[-1]
    _, tree, head = place_of(splits, trees)
    copies = []
    for unit, out in zip(units, outs):
        source = (unit & (trees - 1)) ^ tree
        lanes = pl.ds(pl.multiple_of(((unit >> bits_of(trees)) ^ head) * HEAD_DIM, HEAD_DIM), HEAD_DIM)
        for i, ref in enumerate((key_ref, value_ref)):
            copies.append(pltpu.make_async_copy(ref.at[source, :, lanes], out.at[i], sems.at[len(copies)]))
    for copy in copies:
        copy.start()
    for copy in copies:
        copy.wait()


def project_kernel(splits, trees, heads, states, wq, wk, wv, *targets):
    my_part, my_tree, my_head = place_of(splits, trees)
    share = targets[0].shape[1]
    width = bits_of(splits)
    rows = []
    for part in range(splits):
        for tree in range(trees):
            row = ((tree ^ my_tree) * splits + (reverse_bits(part, width) ^ my_part)) * share
            rows.append(states[pl.ds(pl.multiple_of(row, share), share), :])
    left = jnp.concatenate(rows, 0)
    for head in range(heads):
        source = reverse_bits(head, bits_of(heads)) ^ my_head
        low = 0
        for weight in (wq, wk, wv):
            size = weight.shape[1] // heads
            lanes = pl.ds(pl.multiple_of(source * size, size), size)
            out = jnp.dot(left, weight[:, lanes], preferred_element_type=jnp.float32)
            for group in range(splits * trees):
                spot = group * heads + head
                for target in targets:
                    if spot < target.shape[0]:
                        target[spot, :, low : low + size] = out[group * share : (group + 1) * share]
                        break
                    spot -= target.shape[0]
            low += size


def lane_blocks(value):
    return [value[:, low : low + HEAD_DIM] for low in range(0, value.shape[1], HEAD_DIM)]


def scores_of(query, keys, scores, filled, top):
    def body(i, top):
        piece = dot_t(query[...], keys[i])
        piece = piece + filled[pl.ds(i, 1), :]
        scores[i] = piece
        return functools.reduce(jnp.maximum, lane_blocks(piece), top)

    return lax.fori_loop(0, keys.shape[0], body, top)


def weigh(scores, values, top, mass, acc):
    rate = HEAD_DIM**-0.5 * log2_e

    def body(i, _):
        weight = jnp.exp2((scores[i] - top) * rate)
        mass[...] += functools.reduce(jnp.add, lane_blocks(weight))
        acc[...] += jnp.dot(weight.astype(jnp.bfloat16), values[i], preferred_element_type=jnp.float32)
        return 0

    lax.fori_loop(0, values.shape[0], body, 0)


def cache_kernel(count, group, filled, raw, cosine, sine, *refs):
    chunks = refs[:count]
    query, top_out, mass, acc, keys, values, scores = refs[count:]
    share = raw.shape[0]
    for head in range(group):
        value = raw[:, head * HEAD_DIM : (head + 1) * HEAD_DIM]
        value = value * cosine[...] + pltpu.roll(value, HEAD_DIM // 2, 1) * sine[...]
        query[head * share : (head + 1) * share, :] = value.astype(query.dtype)
    for i, chunk in enumerate(chunks):
        keys[i] = chunk[0]
        values[i] = chunk[1]
    top = jnp.full(top_out.shape, neg_big, jnp.float32)
    top = scores_of(query, keys, scores, filled, top)
    top = jnp.max(top, 1, keepdims=True)
    mass[...] = jnp.zeros(mass.shape, jnp.float32)
    acc[...] = jnp.zeros(acc.shape, jnp.float32)
    weigh(scores, values, top, mass, acc)
    top_out[...] = jnp.broadcast_to(top, top_out.shape)


def last_kernel(count, pieces, group, filled, query, *refs):
    chunks = refs[:count]
    fresh = refs[count : count + pieces]
    bias, top_in, mass_in, acc_in, out, keys, values, scores, nodes, mass, acc = refs[count + pieces :]
    rate = HEAD_DIM**-0.5 * log2_e
    rows = query.shape[0]
    share = rows // group
    for i, chunk in enumerate(chunks):
        keys[i] = chunk[0]
        values[i] = chunk[1]
    mine = lax.axis_index("seq").astype(jnp.int32) & (pieces - 1)
    for i, piece in enumerate(fresh):
        place = pl.ds(pl.multiple_of((mine ^ i) * share, share), share)
        nodes[0, place, :] = piece[0]
        nodes[1, place, :] = piece[1]
    tree = dot_t(query[...], nodes[0])
    tree = (tree.reshape(group, share, -1) + bias[...][None]).reshape(rows, -1)
    top = functools.reduce(jnp.maximum, lane_blocks(tree), top_in[...])
    top = scores_of(query, keys, scores, filled, top)
    top = jnp.max(top, 1, keepdims=True)
    shrink = jnp.exp2((top_in[...] - top) * rate)
    weight = jnp.exp2((tree - top) * rate)
    mass[...] = mass_in[...] * shrink + functools.reduce(jnp.add, lane_blocks(weight))
    acc[...] = acc_in[...] * shrink + jnp.dot(
        weight.astype(jnp.bfloat16), nodes[1], preferred_element_type=jnp.float32
    )
    weigh(scores, values, top, mass, acc)
    total = jnp.sum(mass[...], 1, keepdims=True)
    result = (acc[...] / total).astype(out.dtype)
    for head in range(group):
        out[:, head * HEAD_DIM : (head + 1) * HEAD_DIM] = result[head * share : (head + 1) * share]


def out_kernel(splits, trees, heads, step, *refs):
    my_part, my_tree, my_head = place_of(splits, trees)
    blocks = refs[: splits * trees * heads]
    weight, out = refs[splits * trees * heads :]
    share, depth = blocks[0].shape
    width = out.shape[1]
    if weight.shape[1] == width:
        column = slice(None)
    else:
        column = pl.ds(pl.multiple_of((lax.axis_index("head").astype(jnp.int32) ^ step) * width, width), width)
    total = None
    for head in range(heads):
        left = jnp.concatenate(
            [blocks[(head * trees + tree) * splits + part][...] for tree in range(trees) for part in range(splits)], 0
        )
        deep = pl.ds(pl.multiple_of((head ^ my_head) * depth, depth), depth)
        term = jnp.dot(left, weight[deep, column], preferred_element_type=jnp.float32)
        total = term if total is None else total + term
    for tree in range(trees):
        for part in range(splits):
            row = ((tree ^ my_tree) * splits + (part ^ my_part)) * share
            low = (tree * splits + part) * share
            out[pl.ds(pl.multiple_of(row, share), share), :] = total[low : low + share].astype(out.dtype)


def reach_of(parent):
    count = parent.shape[0]
    spots = jnp.arange(count, dtype=jnp.int32)
    reach = ((parent[:, None] == spots[None, :]) | (spots[:, None] == spots[None, :])).astype(jnp.bfloat16)
    for _ in range(max(1, (count - 1).bit_length())):
        reach = jnp.minimum(jnp.dot(reach, reach, preferred_element_type=jnp.float32), 1.0).astype(jnp.bfloat16)
    return reach.astype(jnp.float32)


def local(size, sides, states, w_query, w_key, w_value, w_out, key_cache, value_cache, parents, cache_lengths):
    trees, tree_rows = parents.shape
    rows = trees * tree_rows
    span = key_cache.shape[1]
    heads = key_cache.shape[2] // HEAD_DIM
    group = w_query.shape[1] // HEAD_DIM // heads
    units = trees * heads
    splits = size // units
    share = tree_rows // splits
    split_bits = bits_of(splits)
    width = (group + 2) * HEAD_DIM
    f32, bf16 = jnp.float32, jnp.bfloat16
    shape = jax.ShapeDtypeStruct

    me = lax.axis_index("seq").astype(jnp.int32)
    side = lax.axis_index("head").astype(jnp.int32)
    my_part = me & (splits - 1)
    my_tree = (me >> split_bits) & (trees - 1)

    steps = bits_of(size)
    pieces = [size // 2, size // 4, size // 4]
    project = pl.pallas_call(
        functools.partial(project_kernel, splits, trees, heads),
        out_shape=[shape((piece, share, width), f32) for piece in pieces],
        in_specs=[VMEM] * 4,
        out_specs=[VMEM] * len(pieces),
        name="project",
        compiler_params=room(12),
    )
    keep, low_send, high_send = project(states, w_query, w_key, w_value)
    rest = None
    for bit in range(steps - 1):
        high = swap(high_send, 1 << bit, size)
        low = swap(low_send, 1 << bit, size)
        if rest is not None:
            high, rest = lax.optimization_barrier((high, rest))
            keep = keep + rest.astype(f32)
        half = keep.shape[0] // 2
        send = (keep[half:] + high.astype(f32)).astype(jnp.float16)
        keep, rest = keep[:half], low
        if bit == 0:
            low, _ = lax.optimization_barrier((low, send[0, :16, :HEAD_DIM]))
            keep, rest = keep + low, None
        low_send, high_send = send[: half // 2], send[half // 2 :]
    high = swap(send, 1 << (steps - 1), size)
    high, rest = lax.optimization_barrier((high, rest))
    raw = (keep + rest.astype(f32) + high.astype(f32))[0]
    away = sorted(range(1, heads), key=lambda h: (h.bit_count() > 1, -h))
    order = [h * trees + t for h in away for t in range(1, trees)]
    order += [h * trees for h in away[:-1]]
    order += list(range(1, trees))
    order += [h * trees for h in away[-1:]]
    held = {}
    first = len(order) // 2
    for some in (order[:first], [0] + order[first:]):
        packed = pl.pallas_call(
            functools.partial(pack_kernel, splits, trees, some),
            out_shape=[shape((2, span, HEAD_DIM), bf16)] * len(some),
            in_specs=[HBM, HBM],
            out_specs=[VMEM] * len(some),
            scratch_shapes=[pltpu.SemaphoreType.DMA((2 * len(some),))],
            name="pack",
            compiler_params=room(60),
        )(key_cache, value_cache)
        for unit, item in zip(some, packed):
            held[unit] = item
            if unit:
                held[unit] = swap(item, unit * splits, size)

    w_out, raw = lax.optimization_barrier((w_out, raw))

    length = lax.dynamic_index_in_dim(cache_lengths, my_tree, 0, False)
    masks = [unit * splits + part for unit in [0] + order for part in range(splits)]
    sources = jnp.stack([me ^ mask for mask in masks])
    places = sources[:, None] * span + jnp.arange(span, dtype=jnp.int32)[None, :]
    filled = jnp.where(places < length, 0.0, neg_big)
    near = len(masks) - splits
    reach = reach_of(lax.dynamic_index_in_dim(parents, my_tree, 0, False))
    reach_rows = lax.dynamic_slice_in_dim(reach, my_part * share, share, 0)
    position = length.astype(f32) + jnp.sum(reach_rows, -1) - 1.0
    half_dim = HEAD_DIM // 2
    freq = rope_base ** (-(jnp.arange(half_dim, dtype=f32) * 2.0 / HEAD_DIM))
    angle = position[:, None] * freq[None, :]
    cosine = jnp.cos(angle)
    sine = jnp.sin(angle)
    cosine = jnp.concatenate([cosine, cosine], -1)
    sine = jnp.concatenate([-sine, sine], -1)
    bias = jnp.where(reach_rows > 0.5, 0.0, neg_big)

    raw_key = raw[:, group * HEAD_DIM : (group + 1) * HEAD_DIM]
    new_key = raw_key * cosine + jnp.roll(raw_key, half_dim, 1) * sine
    fresh = [jnp.stack([new_key.astype(bf16), raw[:, (group + 1) * HEAD_DIM :].astype(bf16)])]
    for bit in range(split_bits):
        fresh = fresh + [swap(item, 1 << bit, size) for item in fresh]
    chunks = []
    for unit in [0] + order:
        pieces = [held[unit]]
        for bit in range(split_bits):
            pieces = pieces + [swap(item, 1 << bit, size) for item in pieces]
        chunks += pieces

    count = group * share
    attend = pl.pallas_call(
        functools.partial(cache_kernel, near, group),
        out_shape=[shape((count, HEAD_DIM), bf16)] + [shape((count, HEAD_DIM), f32)] * 3,
        in_specs=[VMEM] * (4 + near),
        out_specs=[VMEM] * 4,
        scratch_shapes=[
            pltpu.VMEM((near, span, HEAD_DIM), bf16),
            pltpu.VMEM((near, span, HEAD_DIM), bf16),
            pltpu.VMEM((near, count, span), f32),
        ],
        name="cache",
        compiler_params=room(30),
    )
    query, top, mass, acc = attend(filled[:near], raw, cosine, sine, *chunks[:near])

    far = len(masks) - near
    block = pl.pallas_call(
        functools.partial(last_kernel, far, splits, group),
        out_shape=shape((share, group * HEAD_DIM), bf16),
        in_specs=[VMEM] * (2 + far + splits + 4),
        out_specs=VMEM,
        scratch_shapes=[
            pltpu.VMEM((far, span, HEAD_DIM), bf16),
            pltpu.VMEM((far, span, HEAD_DIM), bf16),
            pltpu.VMEM((far, count, span), f32),
            pltpu.VMEM((2, tree_rows, HEAD_DIM), bf16),
            pltpu.VMEM((count, HEAD_DIM), f32),
            pltpu.VMEM((count, HEAD_DIM), f32),
        ],
        name="last",
        compiler_params=room(14),
    )(filled[near:], query, *chunks[near:], *fresh, bias, top, mass, acc)

    blocks = [block] + [swap(block, i * splits * trees, size) for i in range(1, heads)]
    blocks = [
        item if i == 0 else swap(item, i * splits, size) for item in blocks for i in range(trees)
    ]
    blocks = [[item] for item in blocks]
    for bit in range(split_bits):
        blocks = [item + [swap(piece, 1 << bit, size) for piece in item] for item in blocks]
    blocks = [piece for item in blocks for piece in item]

    out_width = w_out.shape[1] // sides
    if sides == 2:
        order = [1, 0]
    else:
        order = list(range(1, sides)) + [0]

    def product(step, dtype):
        weight = w_out
        if out_width % HEAD_DIM:
            weight = lax.dynamic_slice_in_dim(w_out, (side ^ step) * out_width, out_width, 1)
        return pl.pallas_call(
            functools.partial(out_kernel, splits, trees, heads, step),
            out_shape=shape((rows, out_width), dtype),
            in_specs=[VMEM] * (len(blocks) + 1),
            out_specs=VMEM,
            name="output",
            compiler_params=room(12),
        )(*blocks, weight)

    total = None
    arrived = []
    for step in order:
        if step:
            arrived.append(
                lax.ppermute(product(step, bf16), "head", [(i, i ^ step) for i in range(sides)])
            )
        else:
            total = product(step, f32)
    for item in arrived:
        total = total + item.astype(f32)
    return total.astype(bf16)


def solution(mesh):
    placed = (
        P("rep", "seq"),
        P("seq", "head"),
        P("seq", "head"),
        P("seq", "head"),
        P("head", "seq"),
        P("rep", "seq", "head"),
        P("rep", "seq", "head"),
        P("rep", None),
        P("rep"),
    )
    return jax.shard_map(
        functools.partial(local, mesh.shape["seq"], mesh.shape["head"]),
        mesh=mesh,
        in_specs=placed,
        out_specs=P("rep", ("seq", "head")),
        check_vma=False,
    )
```

```python
import functools

import jax
import jax.numpy as jnp
from jax import lax
from jax.experimental import pallas as pl
from jax.experimental.pallas import tpu as pltpu
from jax.sharding import PartitionSpec as P


HEAD_DIM = 128
rope_base = 500000.0
neg_big = -1e30
log2_e = 1.4426950408889634

HBM = pl.BlockSpec(memory_space=pltpu.HBM)
VMEM = pl.BlockSpec(memory_space=pltpu.VMEM)


def room(mib):
    return pltpu.CompilerParams(vmem_limit_bytes=mib * 1024 * 1024)


def bits_of(count):
    return max(0, (count - 1).bit_length())


def reverse_bits(value, width):
    out = 0
    for bit in range(width):
        out = out | (((value >> bit) & 1) << (width - 1 - bit))
    return out


def swap(value, mask, size):
    return lax.ppermute(value, "seq", [(i, i ^ mask) for i in range(size)])


def dot_t(left, right):
    return lax.dot_general(left, right, (((1,), (1,)), ((), ())), preferred_element_type=jnp.float32)


def place_of(splits, trees):
    me = lax.axis_index("seq").astype(jnp.int32)
    split_bits = bits_of(splits)
    return me & (splits - 1), (me >> split_bits) & (trees - 1), me >> (split_bits + bits_of(trees))


def pack_kernel(splits, trees, units, key_ref, value_ref, *refs):
    outs, sems = refs[:-1], refs[-1]
    _, tree, head = place_of(splits, trees)
    copies = []
    for unit, out in zip(units, outs):
        source = (unit & (trees - 1)) ^ tree
        lanes = pl.ds(pl.multiple_of(((unit >> bits_of(trees)) ^ head) * HEAD_DIM, HEAD_DIM), HEAD_DIM)
        for i, ref in enumerate((key_ref, value_ref)):
            copies.append(pltpu.make_async_copy(ref.at[source, :, lanes], out.at[i], sems.at[len(copies)]))
    for copy in copies:
        copy.start()
    for copy in copies:
        copy.wait()


def project_kernel(splits, trees, heads, states, wq, wk, wv, *targets):
    my_part, my_tree, my_head = place_of(splits, trees)
    share = targets[0].shape[1]
    width = bits_of(splits)
    rows = []
    for part in range(splits):
        for tree in range(trees):
            row = ((tree ^ my_tree) * splits + (reverse_bits(part, width) ^ my_part)) * share
            rows.append(states[pl.ds(pl.multiple_of(row, share), share), :])
    left = jnp.concatenate(rows, 0)
    for head in range(heads):
        source = reverse_bits(head, bits_of(heads)) ^ my_head
        low = 0
        for weight in (wq, wk, wv):
            size = weight.shape[1] // heads
            lanes = pl.ds(pl.multiple_of(source * size, size), size)
            out = jnp.dot(left, weight[:, lanes], preferred_element_type=jnp.float32)
            for group in range(splits * trees):
                spot = group * heads + head
                for target in targets:
                    if spot < target.shape[0]:
                        target[spot, :, low : low + size] = out[group * share : (group + 1) * share]
                        break
                    spot -= target.shape[0]
            low += size


def lane_blocks(value):
    return [value[:, low : low + HEAD_DIM] for low in range(0, value.shape[1], HEAD_DIM)]


def scores_of(query, keys, scores, filled, top):
    def body(i, top):
        piece = dot_t(query[...], keys[i])
        piece = piece + filled[pl.ds(i, 1), :]
        scores[i] = piece
        return functools.reduce(jnp.maximum, lane_blocks(piece), top)

    return lax.fori_loop(0, keys.shape[0], body, top, unroll=2)


def weigh(scores, values, top, mass, acc):
    rate = HEAD_DIM**-0.5 * log2_e

    def body(i, _):
        weight = jnp.exp2((scores[i] - top) * rate)
        mass[...] += functools.reduce(jnp.add, lane_blocks(weight))
        acc[...] += jnp.dot(weight.astype(jnp.bfloat16), values[i], preferred_element_type=jnp.float32)
        return 0

    lax.fori_loop(0, values.shape[0], body, 0, unroll=2)


def cache_kernel(count, group, filled, raw, cosine, sine, *refs):
    chunks = refs[:count]
    query, top_out, mass, acc, keys, values, scores = refs[count:]
    share = raw.shape[0]
    for head in range(group):
        value = raw[:, head * HEAD_DIM : (head + 1) * HEAD_DIM]
        value = value * cosine[...] + pltpu.roll(value, HEAD_DIM // 2, 1) * sine[...]
        query[head * share : (head + 1) * share, :] = value.astype(query.dtype)
    for i, chunk in enumerate(chunks):
        keys[i] = chunk[0]
        values[i] = chunk[1]
    top = jnp.full(top_out.shape, neg_big, jnp.float32)
    top = scores_of(query, keys, scores, filled, top)
    top = jnp.max(top, 1, keepdims=True)
    mass[...] = jnp.zeros(mass.shape, jnp.float32)
    acc[...] = jnp.zeros(acc.shape, jnp.float32)
    weigh(scores, values, top, mass, acc)
    top_out[...] = jnp.broadcast_to(top, top_out.shape)


def last_kernel(count, pieces, group, filled, query, *refs):
    chunks = refs[:count]
    fresh = refs[count : count + pieces]
    bias, top_in, mass_in, acc_in, out, keys, values, scores, nodes, mass, acc = refs[count + pieces :]
    rate = HEAD_DIM**-0.5 * log2_e
    rows = query.shape[0]
    share = rows // group
    for i, chunk in enumerate(chunks):
        keys[i] = chunk[0]
        values[i] = chunk[1]
    mine = lax.axis_index("seq").astype(jnp.int32) & (pieces - 1)
    for i, piece in enumerate(fresh):
        place = pl.ds(pl.multiple_of((mine ^ i) * share, share), share)
        nodes[0, place, :] = piece[0]
        nodes[1, place, :] = piece[1]
    tree = dot_t(query[...], nodes[0])
    tree = (tree.reshape(group, share, -1) + bias[...][None]).reshape(rows, -1)
    top = functools.reduce(jnp.maximum, lane_blocks(tree), top_in[...])
    top = scores_of(query, keys, scores, filled, top)
    top = jnp.max(top, 1, keepdims=True)
    shrink = jnp.exp2((top_in[...] - top) * rate)
    weight = jnp.exp2((tree - top) * rate)
    mass[...] = mass_in[...] * shrink + functools.reduce(jnp.add, lane_blocks(weight))
    acc[...] = acc_in[...] * shrink + jnp.dot(
        weight.astype(jnp.bfloat16), nodes[1], preferred_element_type=jnp.float32
    )
    weigh(scores, values, top, mass, acc)
    total = jnp.sum(mass[...], 1, keepdims=True)
    result = (acc[...] / total).astype(out.dtype)
    for head in range(group):
        out[:, head * HEAD_DIM : (head + 1) * HEAD_DIM] = result[head * share : (head + 1) * share]


def out_kernel(splits, trees, heads, step, *refs):
    my_part, my_tree, my_head = place_of(splits, trees)
    blocks = refs[: splits * trees * heads]
    weight, out = refs[splits * trees * heads :]
    share, depth = blocks[0].shape
    width = out.shape[1]
    if weight.shape[1] == width:
        column = slice(None)
    else:
        column = pl.ds(pl.multiple_of((lax.axis_index("head").astype(jnp.int32) ^ step) * width, width), width)
    total = None
    for head in range(heads):
        left = jnp.concatenate(
            [blocks[(head * trees + tree) * splits + part][...] for tree in range(trees) for part in range(splits)], 0
        )
        deep = pl.ds(pl.multiple_of((head ^ my_head) * depth, depth), depth)
        term = jnp.dot(left, weight[deep, column], preferred_element_type=jnp.float32)
        total = term if total is None else total + term
    for tree in range(trees):
        for part in range(splits):
            row = ((tree ^ my_tree) * splits + (part ^ my_part)) * share
            low = (tree * splits + part) * share
            out[pl.ds(pl.multiple_of(row, share), share), :] = total[low : low + share].astype(out.dtype)


def reach_of(parent):
    count = parent.shape[0]
    spots = jnp.arange(count, dtype=jnp.int32)
    reach = ((parent[:, None] == spots[None, :]) | (spots[:, None] == spots[None, :])).astype(jnp.bfloat16)
    for _ in range(max(1, (count - 1).bit_length())):
        reach = jnp.minimum(jnp.dot(reach, reach, preferred_element_type=jnp.float32), 1.0).astype(jnp.bfloat16)
    return reach.astype(jnp.float32)


def local(size, sides, states, w_query, w_key, w_value, w_out, key_cache, value_cache, parents, cache_lengths):
    trees, tree_rows = parents.shape
    rows = trees * tree_rows
    span = key_cache.shape[1]
    heads = key_cache.shape[2] // HEAD_DIM
    group = w_query.shape[1] // HEAD_DIM // heads
    units = trees * heads
    splits = size // units
    share = tree_rows // splits
    split_bits = bits_of(splits)
    width = (group + 2) * HEAD_DIM
    f32, bf16 = jnp.float32, jnp.bfloat16
    shape = jax.ShapeDtypeStruct

    me = lax.axis_index("seq").astype(jnp.int32)
    side = lax.axis_index("head").astype(jnp.int32)
    my_part = me & (splits - 1)
    my_tree = (me >> split_bits) & (trees - 1)

    steps = bits_of(size)
    pieces = [size // 2, size // 4, size // 4]
    project = pl.pallas_call(
        functools.partial(project_kernel, splits, trees, heads),
        out_shape=[shape((piece, share, width), f32) for piece in pieces],
        in_specs=[VMEM] * 4,
        out_specs=[VMEM] * len(pieces),
        name="project",
        compiler_params=room(12),
    )
    keep, low_send, high_send = project(states, w_query, w_key, w_value)
    rest = None
    for bit in range(steps - 1):
        high = swap(high_send, 1 << bit, size)
        low = swap(low_send, 1 << bit, size)
        if rest is not None:
            high, rest = lax.optimization_barrier((high, rest))
            keep = keep + rest.astype(f32)
        half = keep.shape[0] // 2
        send = (keep[half:] + high.astype(f32)).astype(jnp.float16)
        keep, rest = keep[:half], low
        if bit == 0:
            low, _ = lax.optimization_barrier((low, send[0, :16, :HEAD_DIM]))
            keep, rest = keep + low, None
        low_send, high_send = send[: half // 2], send[half // 2 :]
    high = swap(send, 1 << (steps - 1), size)
    high, rest = lax.optimization_barrier((high, rest))
    raw = (keep + rest.astype(f32) + high.astype(f32))[0]
    away = sorted(range(1, heads), key=lambda h: (h.bit_count() > 1, -h))
    order = [h * trees + t for h in away[:-1] for t in range(1, trees)]
    order += [h * trees for h in away[-1:] + away[:-1]]
    order += list(range(1, trees))
    order += [h * trees + t for h in away[-1:] for t in range(1, trees)]
    held = {}
    first = len(order) // 2
    for some in (order[:first], [0] + order[first:]):
        packed = pl.pallas_call(
            functools.partial(pack_kernel, splits, trees, some),
            out_shape=[shape((2, span, HEAD_DIM), bf16)] * len(some),
            in_specs=[HBM, HBM],
            out_specs=[VMEM] * len(some),
            scratch_shapes=[pltpu.SemaphoreType.DMA((2 * len(some),))],
            name="pack",
            compiler_params=room(60),
        )(key_cache, value_cache)
        for unit, item in zip(some, packed):
            held[unit] = item
            if unit:
                held[unit] = swap(item, unit * splits, size)

    w_out, raw = lax.optimization_barrier((w_out, raw))

    length = lax.dynamic_index_in_dim(cache_lengths, my_tree, 0, False)
    masks = [unit * splits + part for unit in [0] + order for part in range(splits)]
    sources = jnp.stack([me ^ mask for mask in masks])
    places = sources[:, None] * span + jnp.arange(span, dtype=jnp.int32)[None, :]
    filled = jnp.where(places < length, 0.0, neg_big)
    near = len(masks) - splits
    reach = reach_of(lax.dynamic_index_in_dim(parents, my_tree, 0, False))
    reach_rows = lax.dynamic_slice_in_dim(reach, my_part * share, share, 0)
    position = length.astype(f32) + jnp.sum(reach_rows, -1) - 1.0
    half_dim = HEAD_DIM // 2
    freq = rope_base ** (-(jnp.arange(half_dim, dtype=f32) * 2.0 / HEAD_DIM))
    angle = position[:, None] * freq[None, :]
    cosine = jnp.cos(angle)
    sine = jnp.sin(angle)
    cosine = jnp.concatenate([cosine, cosine], -1)
    sine = jnp.concatenate([-sine, sine], -1)
    bias = jnp.where(reach_rows > 0.5, 0.0, neg_big)

    raw_key = raw[:, group * HEAD_DIM : (group + 1) * HEAD_DIM]
    new_key = raw_key * cosine + jnp.roll(raw_key, half_dim, 1) * sine
    fresh = [jnp.stack([new_key.astype(bf16), raw[:, (group + 1) * HEAD_DIM :].astype(bf16)])]
    for bit in range(split_bits):
        fresh = fresh + [swap(item, 1 << bit, size) for item in fresh]
    chunks = []
    for unit in [0] + order:
        pieces = [held[unit]]
        for bit in range(split_bits):
            pieces = pieces + [swap(item, 1 << bit, size) for item in pieces]
        chunks += pieces

    count = group * share
    attend = pl.pallas_call(
        functools.partial(cache_kernel, near, group),
        out_shape=[shape((count, HEAD_DIM), bf16)] + [shape((count, HEAD_DIM), f32)] * 3,
        in_specs=[VMEM] * (4 + near),
        out_specs=[VMEM] * 4,
        scratch_shapes=[
            pltpu.VMEM((near, span, HEAD_DIM), bf16),
            pltpu.VMEM((near, span, HEAD_DIM), bf16),
            pltpu.VMEM((near, count, span), f32),
        ],
        name="cache",
        compiler_params=room(30),
    )
    query, top, mass, acc = attend(filled[:near], raw, cosine, sine, *chunks[:near])

    far = len(masks) - near
    block = pl.pallas_call(
        functools.partial(last_kernel, far, splits, group),
        out_shape=shape((share, group * HEAD_DIM), bf16),
        in_specs=[VMEM] * (2 + far + splits + 4),
        out_specs=VMEM,
        scratch_shapes=[
            pltpu.VMEM((far, span, HEAD_DIM), bf16),
            pltpu.VMEM((far, span, HEAD_DIM), bf16),
            pltpu.VMEM((far, count, span), f32),
            pltpu.VMEM((2, tree_rows, HEAD_DIM), bf16),
            pltpu.VMEM((count, HEAD_DIM), f32),
            pltpu.VMEM((count, HEAD_DIM), f32),
        ],
        name="last",
        compiler_params=room(14),
    )(filled[near:], query, *chunks[near:], *fresh, bias, top, mass, acc)

    blocks = [block] + [swap(block, i * splits * trees, size) for i in range(1, heads)]
    blocks = [
        item if i == 0 else swap(item, i * splits, size) for item in blocks for i in range(trees)
    ]
    blocks = [[item] for item in blocks]
    for bit in range(split_bits):
        blocks = [item + [swap(piece, 1 << bit, size) for piece in item] for item in blocks]
    blocks = [piece for item in blocks for piece in item]

    out_width = w_out.shape[1] // sides
    if sides == 2:
        order = [1, 0]
    else:
        order = list(range(1, sides)) + [0]

    def product(step, dtype):
        weight = w_out
        if out_width % HEAD_DIM:
            weight = lax.dynamic_slice_in_dim(w_out, (side ^ step) * out_width, out_width, 1)
        return pl.pallas_call(
            functools.partial(out_kernel, splits, trees, heads, step),
            out_shape=shape((rows, out_width), dtype),
            in_specs=[VMEM] * (len(blocks) + 1),
            out_specs=VMEM,
            name="output",
            compiler_params=room(12),
        )(*blocks, weight)

    total = None
    arrived = []
    for step in order:
        if step:
            arrived.append(
                lax.ppermute(product(step, bf16), "head", [(i, i ^ step) for i in range(sides)])
            )
        else:
            total = product(step, f32)
    for item in arrived:
        total = total + item.astype(f32)
    return total.astype(bf16)


def solution(mesh):
    placed = (
        P("rep", "seq"),
        P("seq", "head"),
        P("seq", "head"),
        P("seq", "head"),
        P("head", "seq"),
        P("rep", "seq", "head"),
        P("rep", "seq", "head"),
        P("rep", None),
        P("rep"),
    )
    return jax.shard_map(
        functools.partial(local, mesh.shape["seq"], mesh.shape["head"]),
        mesh=mesh,
        in_specs=placed,
        out_specs=P("rep", ("seq", "head")),
        check_vma=False,
    )
```
